128 devices in a mesh: group: 8 (over x, y_hi), member: 16 (over y_lo, z, core).
Axes of the slice: x: 4, y: 4 (y_hi: 2, y_lo: 2; y = y_hi * 2 + y_lo), z: 4, core: 2. Of those that a mesh axis runs over, the one named last changes fastest.
Arguments:
- factors: bfloat16 [8, 8192, 8192], P('group', 'member'), as said below
- owner: int32 [1], replicated, may hold values from 0 to 7
- grads: bfloat16 [8192, 1024], P(None, 'group')
Outputs:
- new_factor: bfloat16 [8192, 8192], P('member', 'group')
The draws below stay inside these ranges and needn't reach their ends.
Inputs may be any that keep to these rules, and one draw needn't show every extreme that they name: `owner`: index of the group that owns the updated factor. `factors`: every group's factor is upper triangular with a positive diagonal.
All inputs are finite; a program needn't handle non-finite values.
Results may differ from the reference program's by a relative error of at most 0.0061.
Values may be sent and summed in bfloat16 or wider, within the bound.
No kernel may reach another device: no remote copies, remote signals or barrier semaphores. Data moves between devices by JAX's collectives and lax.ppermute only.
A program may use at most 192 MiB of HBM per device.

```python
import math
import jax
import jax.numpy as jnp
from jax import lax

N = 8192
COLS = 1024
N_GROUP = 8


def draw_factors(key, part):
    noise_key = jax.random.fold_in(key, 11)
    diag_key = jax.random.fold_in(key, 12)
    positions = jnp.arange(N)
    entries = jnp.clip(jax.random.normal(noise_key, (N_GROUP, N, N), jnp.float32), -4.0, 4.0)
    levels = jax.random.uniform(diag_key, (N_GROUP, 1, N), jnp.float32, math.log(0.7), math.log(1.4))
    diag_values = jnp.exp(levels) * (1.0 + 0.35 * positions.astype(jnp.float32) / N)
    above = positions[:, None] < positions[None, :]
    on_diag = positions[:, None] == positions[None, :]
    scaled = entries * (1.5 / math.sqrt(N))
    result = jnp.where(above[None], scaled, jnp.where(on_diag[None], diag_values, 0.0))
    return result.astype(jnp.bfloat16)


def draw_grads(key, part):
    base_key = jax.random.fold_in(key, 21)
    row_key = jax.random.fold_in(key, 22)
    col_key = jax.random.fold_in(key, 23)
    row_scale = jnp.exp(jax.random.uniform(row_key, (N, 1), jnp.float32, math.log(0.5), math.log(2.0)))
    base = jnp.clip(jax.random.normal(base_key, (N, COLS), jnp.float32), -4.0, 4.0)
    col_scale = jnp.exp(jax.random.uniform(col_key, (1, COLS), jnp.float32, math.log(0.3), math.log(3.0)))
    return (base * row_scale * col_scale).astype(jnp.bfloat16)


def setup_inputs(seed: int = 0) -> dict:
    streams_of = jax.random.split(jax.random.key(seed), 4)
    factors = draw_factors(jax.random.fold_in(streams_of[3], 71), 0)
    owner = jax.random.randint(streams_of[1], (1,), 0, N_GROUP).astype(jnp.int32)
    grads = draw_grads(jax.random.fold_in(streams_of[3], 71), 0)
    return dict(factors=factors, owner=owner, grads=grads)


step_size = 1.0


def reference(factors, owner, grads):
    factor = lax.dynamic_index_in_dim(factors, owner[0].astype(jnp.int32), 0, keepdims=False)
    projected = jnp.dot(factor, grads, preferred_element_type=jnp.float32).astype(jnp.bfloat16)
    precond = lax.dot_general(factor, projected, (((0,), (0,)), ((), ())), preferred_element_type=jnp.float32).astype(jnp.bfloat16)
    precond_wide = precond.astype(jnp.float32)
    gram = jnp.dot(precond, precond.T, preferred_element_type=jnp.float32)
    mean_square = jnp.sum(precond_wide * precond_wide) / (N * COLS)
    step_rate = step_size / (1.0 + mean_square)
    factor_wide = factor.astype(jnp.float32)
    combined = jnp.dot(jnp.triu(gram), factor_wide, precision=lax.Precision.HIGHEST)
    updated = (1.0 + step_rate) * factor_wide - (step_rate / COLS) * combined
    return updated.astype(jnp.bfloat16)
```

```python
import jax
import jax.numpy as jnp
from jax import lax
from jax.experimental import pallas as pl
from jax.experimental.pallas import tpu as pltpu
from jax.sharding import Mesh
from jax.sharding import PartitionSpec as P

GROUP = ("x", "yh")
CHIP = ("yl", "z")
MEMBER = ("yl", "z", "core")
GROUP_CHIP = GROUP + CHIP
bf16 = jnp.bfloat16
f32 = jnp.float32
params = pltpu.CompilerParams(vmem_limit_bytes=48 * 1024 * 1024)


def call(body, out, *args, scalars=0, scratch=()):
    vmem = pl.BlockSpec(memory_space=pltpu.VMEM)
    smem = pl.BlockSpec(memory_space=pltpu.SMEM)
    specs = [smem] * scalars + [vmem] * (len(args) - scalars)
    return pl.pallas_call(
        body,
        out_shape=out,
        in_specs=specs,
        out_specs=jax.tree.map(lambda _: vmem, out),
        scratch_shapes=scratch,
        compiler_params=params,
    )(*args)


def shape(dims, dtype=bf16):
    return jax.ShapeDtypeStruct(dims, dtype)


def contract(left, right, a, b):
    return lax.dot_general(left, right, (((a,), (b,)), ((), ())), preferred_element_type=f32)


def joined(ref):
    return jnp.concatenate([ref[b] for b in range(8)], axis=1)


def shift_x(value, step):
    return lax.ppermute(value, "x", [(i, (i + step) % 4) for i in range(4)])


def flip(value, axis):
    return lax.ppermute(value, axis, [(0, 1), (1, 0)])


def copies_to(value, axes):
    return lax.all_to_all(jnp.broadcast_to(value, (8, *value.shape)), axes, 0, 0, tiled=True)


def exchange(tiles, axes):
    return lax.all_to_all(tiles, axes, 0, 0, tiled=True)


def scatter_columns(panel, owner):
    rx = (lax.axis_index("x") - owner // 2) % 4
    ry = (lax.axis_index("yh") - owner % 2) % 2

    def block(i, j):
        g = ((owner // 2 + i) % 4) * 2 + (owner % 2 + j) % 2
        return lax.dynamic_slice_in_dim(panel, g * 1024, 1024, 1)

    to_right = shift_x(block(1, 1), 1)
    to_left = shift_x(block(3, 1), 3)
    across = flip(block(2, 1), "yh")
    far = jnp.where(ry == 0, block(2, 0), across)
    far_right = shift_x(far[:256], 1)
    far_left = shift_x(far[256:], 3)
    across2 = flip(jnp.where(rx == 0, block(0, 1), jnp.where(rx == 1, to_right, to_left)), "yh")
    relay = jnp.concatenate([far_right, far_left], axis=0)
    near_right = shift_x(jnp.where(rx == 0, block(1, 0), relay), 1)
    near_left = shift_x(jnp.where(rx == 0, block(3, 0), relay), 3)
    met = jnp.concatenate([near_right[:256], near_left[256:]], axis=0)
    result = jnp.where(rx == 1, near_right, jnp.where(rx == 3, near_left, met))
    result = jnp.where((ry == 1) & (rx != 2), across2, result)
    return jnp.where((ry == 0) & (rx == 0), block(0, 0), result)


def gradient_rows(grads, member, core):
    piece = lax.dynamic_index_in_dim(grads.reshape(8, 16, 64, 128), member, 1, keepdims=False)
    piece = exchange(piece, GROUP)
    mine = copies_to(piece, CHIP)
    other = flip(mine, "core")
    low = jnp.where(core == 0, mine, other)
    high = jnp.where(core == 0, other, mine)
    rows = jnp.stack([low, high], axis=1)
    return rows.transpose(0, 1, 3, 2, 4).reshape(1024, 1024)


def project_body(a_ref, g_ref, o_ref):
    a = a_ref[...]
    for j in range(4):
        value = jnp.dot(a, g_ref[:, 256 * j : 256 * j + 256], preferred_element_type=f32)
        o_ref[2 * j] = value[:, :128].astype(bf16)
        o_ref[2 * j + 1] = value[:, 128:].astype(bf16)


def spread_body(t_ref, o_ref):
    total = t_ref[0].astype(f32)
    for k in range(1, 8):
        total = total + t_ref[k].astype(f32)
    total = total.astype(bf16)
    for k in range(8):
        o_ref[k] = total


def total_body(t_ref, o_ref):
    total = t_ref[0].astype(f32)
    for k in range(1, 8):
        total = total + t_ref[k].astype(f32)
    o_ref[...] = total.astype(bf16)


def half_of(a_ref, half):
    return a_ref[:, pl.ds(pl.multiple_of(half * 512, 512), 512)]


def give_body(core_ref, a_ref, p_ref, o_ref):
    a = half_of(a_ref, 1 - core_ref[0])
    for j in range(4):
        p = jnp.concatenate([p_ref[2 * j], p_ref[2 * j + 1]], axis=1)
        value = contract(a, p, 0, 0)
        o_ref[2 * j] = value[:, :128].astype(bf16)
        o_ref[2 * j + 1] = value[:, 128:].astype(bf16)


def keep_body(core_ref, a_ref, p_ref, r_ref, o_ref):
    a = half_of(a_ref, core_ref[0])
    for j in range(4):
        p = jnp.concatenate([p_ref[2 * j], p_ref[2 * j + 1]], axis=1)
        value = contract(a, p, 0, 0)
        o_ref[2 * j] = (value[:, :128] + r_ref[2 * j].astype(f32)).astype(bf16)
        o_ref[2 * j + 1] = (value[:, 128:] + r_ref[2 * j + 1].astype(f32)).astype(bf16)


def outer_body(core_ref, q_ref, r_ref, a_ref, b_ref, o_ref):
    a = half_of(a_ref, core_ref[0])
    b = b_ref[...]
    squares = jnp.zeros((8, 128), f32)
    for j in range(4):
        q = jnp.concatenate([q_ref[2 * j], q_ref[2 * j + 1]], axis=1)
        r = jnp.concatenate([r_ref[2 * j], r_ref[2 * j + 1]], axis=1)
        value = (contract(q, a, 0, 0) + contract(r, b, 0, 0)).astype(bf16)
        o_ref[2 * j, :128] = value[:128]
        o_ref[2 * j + 1, :128] = value[128:]
        wide = q.astype(f32)
        squares = squares + jnp.sum((wide * wide).reshape(64, 8, 2, 128), axis=(0, 2))
        wide = r.astype(f32)
        squares = squares + jnp.sum((wide * wide).reshape(64, 8, 2, 128), axis=(0, 2))
    total = jnp.broadcast_to(jnp.sum(squares, axis=(0, 1), keepdims=True), (16, 512))
    top = total.astype(bf16)
    rest = total - top.astype(f32)
    middle = rest.astype(bf16)
    bottom = (rest - middle.astype(f32)).astype(bf16)
    row = lax.broadcasted_iota(jnp.int32, (16, 512), 0)
    tail = jnp.where(row == 0, top.astype(f32), jnp.where(row == 1, middle.astype(f32), bottom.astype(f32)))
    for j in range(8):
        o_ref[j, 128:] = tail.astype(bf16)


def suffix_body(t_ref, o_ref, s_ref):
    total = jnp.zeros((128, 512), f32)
    squares = jnp.zeros((1, 128), f32)
    for k in reversed(range(8)):
        o_ref[k] = total.astype(bf16)
        total = total + t_ref[k, :128].astype(f32)
        tail = t_ref[k, 128:, :128].astype(f32)
        squares = squares + (tail[0:1] + tail[1:2] + tail[2:3])
    s_ref[...] = jnp.broadcast_to(squares, (8, 128))


def near_body(core_ref, q_ref, r_ref, a_ref, b_ref, o_ref):
    core = core_ref[0]
    q = joined(q_ref)
    r = joined(r_ref)
    a = half_of(a_ref, core)
    b = b_ref[...]
    upper = lax.broadcasted_iota(jnp.int32, (512, 512), 0) <= lax.broadcasted_iota(jnp.int32, (512, 512), 1)
    o_ref[0] = jnp.dot(jnp.where(upper, contract(q, q, 1, 1), 0.0).astype(bf16), a, preferred_element_type=f32)
    o_ref[1] = jnp.dot(jnp.where(upper, contract(r, r, 1, 1), 0.0).astype(bf16), b, preferred_element_type=f32)

    @pl.when(core == 0)
    def _():
        o_ref[0] += jnp.dot(contract(q, r, 1, 1).astype(bf16), b, preferred_element_type=f32)

    @pl.when(core == 1)
    def _():
        o_ref[1] += jnp.dot(contract(r, q, 1, 1).astype(bf16), a, preferred_element_type=f32)


def update_body(core_ref, q_ref, r_ref, s_ref, n_ref, a_ref, b_ref, m_ref, o_ref, p_ref):
    a = half_of(a_ref, core_ref[0])
    b = b_ref[...]
    s = s_ref[...].reshape(1024, 512)
    rate = 1.0 / (1.0 + m_ref[0:1, 0:1] * (1.0 / 8388608.0))
    for ref, out, base, k in ((q_ref, o_ref, a, 0), (r_ref, p_ref, b, 1)):
        combined = n_ref[k] + jnp.dot(joined(ref), s, preferred_element_type=f32)
        out[...] = ((1.0 + rate) * base.astype(f32) - (rate * (1.0 / 1024.0)) * combined).astype(bf16)


def shards(factors, owner, grads):
    core = lax.axis_index("core")
    cores = core[None].astype(jnp.int32)
    member = lax.axis_index(MEMBER)
    own = scatter_columns(factors[0], owner[0])
    rows = gradient_rows(grads, member, core)
    tiles = shape((8, 512, 128))
    projected = call(project_body, tiles, own, rows)
    projected = exchange(projected, GROUP)
    projected = exchange(call(spread_body, tiles, projected), GROUP)
    given = flip(call(give_body, tiles, cores, own, projected, scalars=1), "core")
    kept = call(keep_body, tiles, cores, own, projected, given, scalars=1)
    other_own = flip(lax.dynamic_slice_in_dim(own, (1 - core) * 512, 512, 1), "core")
    piece = call(total_body, shape((512, 128)), exchange(kept, CHIP))
    swap = []
    for x in range(4):
        for yh in range(2):
            for yl in range(2):
                for z in range(4):
                    g, c = x * 2 + yh, yl * 4 + z
                    swap.append((g * 8 + c, c * 8 + g))
    piece = lax.ppermute(piece, GROUP_CHIP, swap)
    precond = copies_to(piece, GROUP)
    other = flip(precond, "core")
    products = call(outer_body, shape((8, 144, 512)), cores, precond, other, own, other_own, scalars=1)
    near = call(near_body, shape((2, 512, 512), f32), cores, precond, other, own, other_own, scalars=1)
    products = exchange(products, CHIP)
    later, squares = call(suffix_body, (shape((8, 128, 512)), shape((8, 128), f32)), products)
    later = exchange(later, CHIP)
    half = shape((512, 512))
    mine, theirs = call(
        update_body, (half, half), cores, precond, other, later, near, own, other_own, squares, scalars=1
    )
    theirs = flip(theirs, "core")
    left = jnp.where(core == 0, mine, theirs)
    right = jnp.where(core == 0, theirs, mine)
    return jnp.concatenate([left, right], axis=1)


def solution(mesh):
    split = Mesh(mesh.devices.reshape(4, 2, 2, 4, 2), GROUP + MEMBER)
    in_specs = (P(GROUP, MEMBER, None), P(), P(None, GROUP))
    out_specs = P(MEMBER, GROUP)
    return jax.shard_map(shards, mesh=split, in_specs=in_specs, out_specs=out_specs, check_vma=False)
```

```python
import jax
import jax.numpy as jnp
from jax import lax
from jax.experimental import pallas as pl
from jax.experimental.pallas import tpu as pltpu
from jax.sharding import Mesh
from jax.sharding import PartitionSpec as P

GROUP = ("x", "yh")
CHIP = ("yl", "z")
MEMBER = ("yl", "z", "core")
GROUP_CHIP = GROUP + CHIP
bf16 = jnp.bfloat16
f32 = jnp.float32
params = pltpu.CompilerParams(vmem_limit_bytes=48 * 1024 * 1024)


def call(body, out, *args, scalars=0, scratch=()):
    vmem = pl.BlockSpec(memory_space=pltpu.VMEM)
    smem = pl.BlockSpec(memory_space=pltpu.SMEM)
    specs = [smem] * scalars + [vmem] * (len(args) - scalars)
    return pl.pallas_call(
        body,
        out_shape=out,
        in_specs=specs,
        out_specs=jax.tree.map(lambda _: vmem, out),
        scratch_shapes=scratch,
        compiler_params=params,
    )(*args)


def shape(dims, dtype=bf16):
    return jax.ShapeDtypeStruct(dims, dtype)


def contract(left, right, a, b):
    return lax.dot_general(left, right, (((a,), (b,)), ((), ())), preferred_element_type=f32)


def joined(ref):
    return jnp.concatenate([ref[b] for b in range(8)], axis=1)


def shift_x(value, step):
    return lax.ppermute(value, "x", [(i, (i + step) % 4) for i in range(4)])


def flip(value, axis):
    return lax.ppermute(value, axis, [(0, 1), (1, 0)])


def copies_to(value, axes):
    return lax.all_to_all(jnp.broadcast_to(value, (8, *value.shape)), axes, 0, 0, tiled=True)


def exchange(tiles, axes):
    return lax.all_to_all(tiles, axes, 0, 0, tiled=True)


def copy_blocks(panel_ref, sems, *pairs):
    copies = []
    for column, out_ref in pairs:
        start = pl.multiple_of(column * 1024, 1024)
        for top in (0, 128, 256, 384):
            source = panel_ref.at[pl.ds(top, 128), pl.ds(start, 1024)]
            copies.append(pltpu.make_async_copy(source, out_ref.at[pl.ds(top, 128)], sems.at[len(copies)]))
    for copy in copies:
        copy.start()
    for copy in copies:
        copy.wait()


FAR, DOWN, RIGHT, LEFT, HERE, CORE = 2, 3, 4, 5, 6, 7


def second_body(plan_ref, panel_ref, right_ref, left_ref, across_ref, upper_ref, lower_ref, cross_ref, far_ref, sems):
    column, row = plan_ref[0], plan_ref[1]

    @pl.when((column == 0) & (row == 0))
    def _():
        copy_blocks(panel_ref, sems, (plan_ref[FAR], far_ref), (plan_ref[DOWN], cross_ref))
        upper_ref[...] = far_ref[:256]
        lower_ref[...] = far_ref[256:]

    @pl.when((column != 0) | (row != 0))
    def _():
        upper_ref[...] = across_ref[:256]
        lower_ref[...] = across_ref[256:]

    @pl.when(column == 1)
    def _():
        cross_ref[...] = right_ref[...]

    @pl.when((column != 1) & ((column != 0) | (row != 0)))
    def _():
        cross_ref[...] = left_ref[...]


def third_body(plan_ref, panel_ref, right_ref, left_ref, to_right_ref, to_left_ref, sems):
    @pl.when(plan_ref[0] == 0)
    def _():
        copy_blocks(panel_ref, sems, (plan_ref[RIGHT], to_right_ref), (plan_ref[LEFT], to_left_ref))

    @pl.when(plan_ref[0] > 0)
    def _():
        for ref in (to_right_ref, to_left_ref):
            ref[:256] = right_ref[...]
            ref[256:] = left_ref[...]


def with_panel(body, out, plan, panel, *received, scratch=()):
    vmem = pl.BlockSpec(memory_space=pltpu.VMEM)
    return pl.pallas_call(
        body,
        out_shape=out,
        in_specs=[pl.BlockSpec(memory_space=pltpu.SMEM), pl.BlockSpec(memory_space=pl.ANY)] + [vmem] * len(received),
        out_specs=jax.tree.map(lambda _: vmem, out),
        scratch_shapes=(*scratch, pltpu.SemaphoreType.DMA((8,))),
        compiler_params=params,
    )(plan, panel, *received)


def scatter_columns(panel, owner):
    rx = (lax.axis_index("x") - owner // 2) % 4
    ry = (lax.axis_index("yh") - owner % 2) % 2

    def column(i, j):
        return ((owner // 2 + i) % 4) * 2 + (owner % 2 + j) % 2

    def block(i, j):
        return lax.dynamic_slice_in_dim(panel, column(i, j) * 1024, 1024, 1)

    places = [column(2, 0), column(0, 1), column(1, 0), column(3, 0), column(0, 0)]
    plan = jnp.stack([rx, ry, *places, lax.axis_index("core")]).astype(jnp.int32)
    full, half = shape((512, 1024)), shape((256, 1024))
    to_right = shift_x(block(1, 1), 1)
    to_left = shift_x(block(3, 1), 3)
    across = flip(block(2, 1), "yh")
    upper, lower, crossing = with_panel(
        second_body, (half, half, full), plan, panel, to_right, to_left, across,
        scratch=(pltpu.VMEM((512, 1024), bf16),),
    )
    across = flip(crossing, "yh")
    far_right = shift_x(upper, 1)
    far_left = shift_x(lower, 3)
    near_right, near_left = with_panel(third_body, (full, full), plan, panel, far_right, far_left)
    return plan, (shift_x(near_right, 1), shift_x(near_left, 3), across)


def half_body(core_ref, g_ref, o_ref):
    pltpu.sync_copy(g_ref.at[:, core_ref[0]], o_ref)


def gradient_half(grads, cores):
    return pl.pallas_call(
        half_body,
        out_shape=shape((8, 512, 128)),
        in_specs=[pl.BlockSpec(memory_space=pltpu.SMEM), pl.BlockSpec(memory_space=pl.ANY)],
        out_specs=pl.BlockSpec(memory_space=pltpu.VMEM),
    )(cores, grads.reshape(8, 2, 512, 128))


def project_body(plan_ref, panel_ref, g_ref, h_ref, right_ref, left_ref, across_ref, a_ref, o_ref, sems):
    column, row = plan_ref[0], plan_ref[1]
    straight = row == 0

    @pl.when((column == 0) & straight)
    def _():
        copy_blocks(panel_ref, sems, (plan_ref[HERE], a_ref))

    @pl.when((column == 1) & straight)
    def _():
        a_ref[...] = right_ref[...]

    @pl.when((column == 3) & straight)
    def _():
        a_ref[...] = left_ref[...]

    @pl.when(column == 2)
    def _():
        a_ref[:256] = right_ref[:256]
        a_ref[256:] = left_ref[256:]

    @pl.when((column != 2) & (row == 1))
    def _():
        a_ref[...] = across_ref[...]

    mine, other = half_of(a_ref, plan_ref[CORE]), half_of(a_ref, 1 - plan_ref[CORE])
    for j in range(4):
        g = jnp.concatenate([g_ref[2 * j], g_ref[2 * j + 1]], axis=1)
        h = jnp.concatenate([h_ref[2 * j], h_ref[2 * j + 1]], axis=1)
        value = jnp.dot(mine, g, preferred_element_type=f32) + jnp.dot(other, h, preferred_element_type=f32)
        o_ref[2 * j] = value[:, :128].astype(bf16)
        o_ref[2 * j + 1] = value[:, 128:].astype(bf16)


def spread_body(t_ref, o_ref):
    total = t_ref[0].astype(f32)
    for k in range(1, 8):
        total = total + t_ref[k].astype(f32)
    total = total.astype(bf16)
    for k in range(8):
        o_ref[k] = total


def total_body(t_ref, o_ref):
    total = t_ref[0].astype(f32)
    for k in range(1, 8):
        total = total + t_ref[k].astype(f32)
    o_ref[...] = total.astype(bf16)


def half_of(a_ref, half):
    return a_ref[:, pl.ds(pl.multiple_of(half * 512, 512), 512)]


def give_body(core_ref, a_ref, p_ref, o_ref):
    a = half_of(a_ref, 1 - core_ref[0])
    for j in range(4):
        p = jnp.concatenate([p_ref[2 * j], p_ref[2 * j + 1]], axis=1)
        value = contract(a, p, 0, 0)
        o_ref[2 * j] = value[:, :128].astype(bf16)
        o_ref[2 * j + 1] = value[:, 128:].astype(bf16)


def keep_body(core_ref, a_ref, p_ref, r_ref, o_ref):
    a = half_of(a_ref, core_ref[0])
    for j in range(4):
        p = jnp.concatenate([p_ref[2 * j], p_ref[2 * j + 1]], axis=1)
        value = contract(a, p, 0, 0)
        o_ref[2 * j] = (value[:, :128] + r_ref[2 * j].astype(f32)).astype(bf16)
        o_ref[2 * j + 1] = (value[:, 128:] + r_ref[2 * j + 1].astype(f32)).astype(bf16)


def outer_body(core_ref, q_ref, r_ref, a_ref, b_ref, o_ref):
    a = half_of(a_ref, core_ref[0])
    b = b_ref[...]
    squares = jnp.zeros((8, 128), f32)
    for j in range(4):
        q = jnp.concatenate([q_ref[2 * j], q_ref[2 * j + 1]], axis=1)
        r = jnp.concatenate([r_ref[2 * j], r_ref[2 * j + 1]], axis=1)
        value = (contract(q, a, 0, 0) + contract(r, b, 0, 0)).astype(bf16)
        o_ref[2 * j, :128] = value[:128]
        o_ref[2 * j + 1, :128] = value[128:]
        wide = q.astype(f32)
        squares = squares + jnp.sum((wide * wide).reshape(64, 8, 2, 128), axis=(0, 2))
        wide = r.astype(f32)
        squares = squares + jnp.sum((wide * wide).reshape(64, 8, 2, 128), axis=(0, 2))
    total = jnp.broadcast_to(jnp.sum(squares, axis=(0, 1), keepdims=True), (16, 512))
    top = total.astype(bf16)
    rest = total - top.astype(f32)
    middle = rest.astype(bf16)
    bottom = (rest - middle.astype(f32)).astype(bf16)
    row = lax.broadcasted_iota(jnp.int32, (16, 512), 0)
    tail = jnp.where(row == 0, top.astype(f32), jnp.where(row == 1, middle.astype(f32), bottom.astype(f32)))
    for j in range(8):
        o_ref[j, 128:] = tail.astype(bf16)


def suffix_body(t_ref, o_ref, s_ref):
    total = jnp.zeros((128, 512), f32)
    squares = jnp.zeros((1, 128), f32)
    for k in reversed(range(8)):
        o_ref[k] = total.astype(bf16)
        total = total + t_ref[k, :128].astype(f32)
        tail = t_ref[k, 128:, :128].astype(f32)
        squares = squares + (tail[0:1] + tail[1:2] + tail[2:3])
    s_ref[...] = jnp.broadcast_to(squares, (8, 128))


def near_body(core_ref, q_ref, r_ref, a_ref, b_ref, o_ref):
    core = core_ref[0]
    q = joined(q_ref)
    r = joined(r_ref)
    a = half_of(a_ref, core)
    b = b_ref[...]

    def times(gram, rows):
        top = gram.astype(bf16)
        rest = (gram - top.astype(f32)).astype(bf16)
        return jnp.dot(top, rows, preferred_element_type=f32) + jnp.dot(rest, rows, preferred_element_type=f32)

    upper = lax.broadcasted_iota(jnp.int32, (512, 512), 0) <= lax.broadcasted_iota(jnp.int32, (512, 512), 1)
    o_ref[0] = times(jnp.where(upper, contract(q, q, 1, 1), 0.0), a)
    o_ref[1] = times(jnp.where(upper, contract(r, r, 1, 1), 0.0), b)

    @pl.when(core == 0)
    def _():
        o_ref[0] += times(contract(q, r, 1, 1), b)

    @pl.when(core == 1)
    def _():
        o_ref[1] += times(contract(r, q, 1, 1), a)


def update_body(core_ref, q_ref, r_ref, s_ref, n_ref, a_ref, b_ref, m_ref, o_ref, p_ref):
    a = half_of(a_ref, core_ref[0])
    b = b_ref[...]
    s = s_ref[...].reshape(1024, 512)
    rate = 1.0 / (1.0 + m_ref[0:1, 0:1] * (1.0 / 8388608.0))
    for ref, out, base, k in ((q_ref, o_ref, a, 0), (r_ref, p_ref, b, 1)):
        combined = n_ref[k] + jnp.dot(joined(ref), s, preferred_element_type=f32)
        out[...] = ((1.0 + rate) * base.astype(f32) - (rate * (1.0 / 1024.0)) * combined).astype(bf16)


def shards(factors, owner, grads):
    core = lax.axis_index("core")
    cores = core[None].astype(jnp.int32)
    mine = exchange(gradient_half(grads, cores), GROUP)
    plan, received = scatter_columns(factors[0], owner[0])
    tiles = shape((8, 512, 128))
    own, projected = with_panel(project_body, (shape((512, 1024)), tiles), plan, factors[0], mine, flip(mine, "core"), *received)
    projected = exchange(projected, GROUP)
    projected = exchange(call(spread_body, tiles, projected), GROUP)
    given = flip(call(give_body, tiles, cores, own, projected, scalars=1), "core")
    kept = call(keep_body, tiles, cores, own, projected, given, scalars=1)
    other_own = flip(lax.dynamic_slice_in_dim(own, (1 - core) * 512, 512, 1), "core")
    piece = call(total_body, shape((512, 128)), exchange(kept, CHIP))
    swap = []
    for x in range(4):
        for yh in range(2):
            for yl in range(2):
                for z in range(4):
                    g, c = x * 2 + yh, yl * 4 + z
                    swap.append((g * 8 + c, c * 8 + g))
    piece = lax.ppermute(piece, GROUP_CHIP, swap)
    precond = copies_to(piece, GROUP)
    other = flip(precond, "core")
    products = call(outer_body, shape((8, 144, 512)), cores, precond, other, own, other_own, scalars=1)
    near = call(near_body, shape((2, 512, 512), f32), cores, precond, other, own, other_own, scalars=1)
    products = exchange(products, CHIP)
    later, squares = call(suffix_body, (shape((8, 128, 512)), shape((8, 128), f32)), products)
    later = exchange(later, CHIP)
    half = shape((512, 512))
    mine, theirs = call(
        update_body, (half, half), cores, precond, other, later, near, own, other_own, squares, scalars=1
    )
    theirs = flip(theirs, "core")
    left = jnp.where(core == 0, mine, theirs)
    right = jnp.where(core == 0, theirs, mine)
    return jnp.concatenate([left, right], axis=1)


def solution(mesh):
    split = Mesh(mesh.devices.reshape(4, 2, 2, 4, 2), GROUP + MEMBER)
    in_specs = (P(GROUP, MEMBER, None), P(), P(None, GROUP))
    out_specs = P(MEMBER, GROUP)
    return jax.shard_map(shards, mesh=split, in_specs=in_specs, out_specs=out_specs, check_vma=False)
```

```python
import jax
import jax.numpy as jnp
from jax import lax
from jax.experimental import pallas as pl
from jax.experimental.pallas import tpu as pltpu
from jax.sharding import Mesh
from jax.sharding import PartitionSpec as P

GROUP = ("x", "yh")
CHIP = ("yl", "z")
MEMBER = ("yl", "z", "core")
GROUP_CHIP = GROUP + CHIP
bf16 = jnp.bfloat16
f32 = jnp.float32
params = pltpu.CompilerParams(vmem_limit_bytes=48 * 1024 * 1024)


def call(body, out, *args, scalars=0, scratch=()):
    vmem = pl.BlockSpec(memory_space=pltpu.VMEM)
    smem = pl.BlockSpec(memory_space=pltpu.SMEM)
    specs = [smem] * scalars + [vmem] * (len(args) - scalars)
    return pl.pallas_call(
        body,
        out_shape=out,
        in_specs=specs,
        out_specs=jax.tree.map(lambda _: vmem, out),
        scratch_shapes=scratch,
        compiler_params=params,
    )(*args)


def shape(dims, dtype=bf16):
    return jax.ShapeDtypeStruct(dims, dtype)


def contract(left, right, a, b):
    return lax.dot_general(left, right, (((a,), (b,)), ((), ())), preferred_element_type=f32)


def joined(ref):
    return jnp.concatenate([ref[b] for b in range(8)], axis=1)


def shift_x(value, step):
    return lax.ppermute(value, "x", [(i, (i + step) % 4) for i in range(4)])


def flip(value, axis):
    return lax.ppermute(value, axis, [(0, 1), (1, 0)])


def copies_to(value, axes):
    return lax.all_to_all(jnp.broadcast_to(value, (8, *value.shape)), axes, 0, 0, tiled=True)


def exchange(tiles, axes):
    return lax.all_to_all(tiles, axes, 0, 0, tiled=True)


def copy_blocks(panel_ref, sems, *pairs):
    copies = []
    for column, out_ref in pairs:
        start = pl.multiple_of(column * 1024, 1024)
        for top in range(0, out_ref.shape[0], 128):
            source = panel_ref.at[pl.ds(top, 128), pl.ds(start, 1024)]
            copies.append(pltpu.make_async_copy(source, out_ref.at[pl.ds(top, 128)], sems.at[len(copies)]))
    for copy in copies:
        copy.start()
    for copy in copies:
        copy.wait()


FAR, DOWN, RIGHT, LEFT, HERE, QUARTER = 2, 3, 4, 5, 6, 7


def cross_body(plan_ref, panel_ref, right_ref, left_ref, cross_ref, sems):
    @pl.when(plan_ref[0] == 0)
    def _():
        copy_blocks(panel_ref, sems, (plan_ref[DOWN], cross_ref))

    @pl.when(plan_ref[0] == 1)
    def _():
        cross_ref[...] = right_ref[...]

    @pl.when(plan_ref[0] > 1)
    def _():
        cross_ref[...] = left_ref[...]


def far_body(plan_ref, panel_ref, across_ref, upper_ref, lower_ref, far_ref, sems):
    @pl.when(plan_ref[1] == 0)
    def _():
        copy_blocks(panel_ref, sems, (plan_ref[FAR], far_ref))
        upper_ref[...] = far_ref[:256]
        lower_ref[...] = far_ref[256:]

    @pl.when(plan_ref[1] == 1)
    def _():
        upper_ref[...] = across_ref[:256]
        lower_ref[...] = across_ref[256:]


def third_body(plan_ref, panel_ref, right_ref, left_ref, to_right_ref, to_left_ref, sems):
    @pl.when(plan_ref[0] == 0)
    def _():
        copy_blocks(panel_ref, sems, (plan_ref[RIGHT], to_right_ref), (plan_ref[LEFT], to_left_ref))

    @pl.when(plan_ref[0] > 0)
    def _():
        to_right_ref[...] = right_ref[...]
        to_left_ref[...] = left_ref[...]


def with_panel(body, out, plan, panel, *received, scratch=()):
    vmem = pl.BlockSpec(memory_space=pltpu.VMEM)
    return pl.pallas_call(
        body,
        out_shape=out,
        in_specs=[pl.BlockSpec(memory_space=pltpu.SMEM), pl.BlockSpec(memory_space=pl.ANY)] + [vmem] * len(received),
        out_specs=jax.tree.map(lambda _: vmem, out),
        scratch_shapes=(*scratch, pltpu.SemaphoreType.DMA((8,))),
        compiler_params=params,
    )(plan, panel, *received)


def scatter_columns(panel, owner, quarter):
    rx = (lax.axis_index("x") - owner // 2) % 4
    ry = (lax.axis_index("yh") - owner % 2) % 2

    def column(i, j):
        return ((owner // 2 + i) % 4) * 2 + (owner % 2 + j) % 2

    def block(i, j):
        return lax.dynamic_slice_in_dim(panel, column(i, j) * 1024, 1024, 1)

    places = [column(2, 0), column(0, 1), column(1, 0), column(3, 0), column(0, 0)]
    plan = jnp.stack([rx, ry, *places, quarter]).astype(jnp.int32)
    full, half = shape((512, 1024)), shape((256, 1024))
    to_right = shift_x(block(1, 1), 1)
    to_left = shift_x(block(3, 1), 3)
    across = flip(block(2, 1), "yh")
    lower_right = shift_x(block(1, 0)[256:], 1)
    lower_left = shift_x(block(3, 0)[256:], 3)
    crossing = flip(with_panel(cross_body, full, plan, panel, to_right, to_left), "yh")
    upper, lower = with_panel(
        far_body, (half, half), plan, panel, across, scratch=(pltpu.VMEM((512, 1024), bf16),)
    )
    far_right = shift_x(upper, 1)
    far_left = shift_x(lower, 3)
    upper_right, upper_left = with_panel(third_body, (half, half), plan, panel, far_right, far_left)
    return plan, (shift_x(upper_right, 1), lower_right, shift_x(upper_left, 3), lower_left, crossing)


def quarter_body(plan_ref, g_ref, o_ref):
    pltpu.sync_copy(g_ref.at[:, plan_ref[0]], o_ref)


def gradient_quarters(grads, quarter):
    piece = pl.pallas_call(
        quarter_body,
        out_shape=shape((8, 256, 128)),
        in_specs=[pl.BlockSpec(memory_space=pltpu.SMEM), pl.BlockSpec(memory_space=pl.ANY)],
        out_specs=pl.BlockSpec(memory_space=pltpu.VMEM),
    )(quarter[None].astype(jnp.int32), grads.reshape(8, 4, 256, 128))
    mine = exchange(piece, GROUP)
    near = lax.ppermute(mine, "z", [(0, 1), (1, 0), (2, 3), (3, 2)])
    return mine, near, flip(mine, "core"), flip(near, "core")


def project_body(plan_ref, panel_ref, g0_ref, g1_ref, g2_ref, g3_ref, *refs):
    upper_right, lower_right, upper_left, lower_left, across_ref, a_ref, o_ref, sems = refs
    column, row = plan_ref[0], plan_ref[1]
    straight = row == 0

    @pl.when((column == 0) & straight)
    def _():
        copy_blocks(panel_ref, sems, (plan_ref[HERE], a_ref))

    @pl.when((column == 1) & straight)
    def _():
        a_ref[:256] = upper_right[...]
        a_ref[256:] = lower_right[...]

    @pl.when((column == 3) & straight)
    def _():
        a_ref[:256] = upper_left[...]
        a_ref[256:] = lower_left[...]

    @pl.when(column == 2)
    def _():
        a_ref[:256] = upper_right[...]
        a_ref[256:] = upper_left[...]

    @pl.when((column != 2) & (row == 1))
    def _():
        a_ref[...] = across_ref[...]

    quarter = plan_ref[QUARTER]
    half = 2 * (quarter // 2)
    place = quarter - half
    columns = (quarter, half + 1 - place, 2 - half + place, 2 - half + 1 - place)
    parts = [a_ref[:, pl.ds(pl.multiple_of(k * 256, 256), 256)] for k in columns]
    for j in range(4):
        value = jnp.zeros((512, 256), f32)
        for part, ref in zip(parts, (g0_ref, g1_ref, g2_ref, g3_ref)):
            rows = jnp.concatenate([ref[2 * j], ref[2 * j + 1]], axis=1)
            value = value + jnp.dot(part, rows, preferred_element_type=f32)
        o_ref[2 * j] = value[:, :128].astype(bf16)
        o_ref[2 * j + 1] = value[:, 128:].astype(bf16)


def spread_body(t_ref, o_ref):
    total = t_ref[0].astype(f32)
    for k in range(1, 8):
        total = total + t_ref[k].astype(f32)
    total = total.astype(bf16)
    for k in range(8):
        o_ref[k] = total


def total_body(t_ref, o_ref):
    total = t_ref[0].astype(f32)
    for k in range(1, 8):
        total = total + t_ref[k].astype(f32)
    o_ref[...] = total.astype(bf16)


def half_of(a_ref, half):
    return a_ref[:, pl.ds(pl.multiple_of(half * 512, 512), 512)]


def give_body(core_ref, a_ref, p_ref, o_ref):
    a = half_of(a_ref, 1 - core_ref[0])
    for j in range(4):
        p = jnp.concatenate([p_ref[2 * j], p_ref[2 * j + 1]], axis=1)
        value = contract(a, p, 0, 0)
        o_ref[2 * j] = value[:, :128].astype(bf16)
        o_ref[2 * j + 1] = value[:, 128:].astype(bf16)


def keep_body(core_ref, a_ref, p_ref, r_ref, o_ref):
    a = half_of(a_ref, core_ref[0])
    for j in range(4):
        p = jnp.concatenate([p_ref[2 * j], p_ref[2 * j + 1]], axis=1)
        value = contract(a, p, 0, 0)
        o_ref[2 * j] = (value[:, :128] + r_ref[2 * j].astype(f32)).astype(bf16)
        o_ref[2 * j + 1] = (value[:, 128:] + r_ref[2 * j + 1].astype(f32)).astype(bf16)


def outer_body(core_ref, q_ref, r_ref, a_ref, b_ref, o_ref):
    a = half_of(a_ref, core_ref[0])
    b = b_ref[...]
    squares = jnp.zeros((8, 128), f32)
    for j in range(4):
        q = jnp.concatenate([q_ref[2 * j], q_ref[2 * j + 1]], axis=1)
        r = jnp.concatenate([r_ref[2 * j], r_ref[2 * j + 1]], axis=1)
        value = (contract(q, a, 0, 0) + contract(r, b, 0, 0)).astype(bf16)
        o_ref[2 * j, :128] = value[:128]
        o_ref[2 * j + 1, :128] = value[128:]
        wide = q.astype(f32)
        squares = squares + jnp.sum((wide * wide).reshape(64, 8, 2, 128), axis=(0, 2))
        wide = r.astype(f32)
        squares = squares + jnp.sum((wide * wide).reshape(64, 8, 2, 128), axis=(0, 2))
    total = jnp.broadcast_to(jnp.sum(squares, axis=(0, 1), keepdims=True), (16, 512))
    top = total.astype(bf16)
    rest = total - top.astype(f32)
    middle = rest.astype(bf16)
    bottom = (rest - middle.astype(f32)).astype(bf16)
    row = lax.broadcasted_iota(jnp.int32, (16, 512), 0)
    tail = jnp.where(row == 0, top.astype(f32), jnp.where(row == 1, middle.astype(f32), bottom.astype(f32)))
    for j in range(8):
        o_ref[j, 128:] = tail.astype(bf16)


def suffix_body(t_ref, o_ref, s_ref):
    total = jnp.zeros((128, 512), f32)
    squares = jnp.zeros((1, 128), f32)
    for k in reversed(range(8)):
        o_ref[k] = total.astype(bf16)
        total = total + t_ref[k, :128].astype(f32)
        tail = t_ref[k, 128:, :128].astype(f32)
        squares = squares + (tail[0:1] + tail[1:2] + tail[2:3])
    s_ref[...] = jnp.broadcast_to(squares, (8, 128))


def near_body(core_ref, q_ref, r_ref, a_ref, b_ref, o_ref):
    core = core_ref[0]
    q = joined(q_ref)
    r = joined(r_ref)
    a = half_of(a_ref, core)
    b = b_ref[...]

    def times(gram, rows):
        top = gram.astype(bf16)
        rest = (gram - top.astype(f32)).astype(bf16)
        return jnp.dot(top, rows, preferred_element_type=f32) + jnp.dot(rest, rows, preferred_element_type=f32)

    upper = lax.broadcasted_iota(jnp.int32, (512, 512), 0) <= lax.broadcasted_iota(jnp.int32, (512, 512), 1)
    o_ref[0] = times(jnp.where(upper, contract(q, q, 1, 1), 0.0), a)
    o_ref[1] = times(jnp.where(upper, contract(r, r, 1, 1), 0.0), b)

    @pl.when(core == 0)
    def _():
        o_ref[0] += times(contract(q, r, 1, 1), b)

    @pl.when(core == 1)
    def _():
        o_ref[1] += times(contract(r, q, 1, 1), a)


def update_body(core_ref, q_ref, r_ref, s_ref, n_ref, a_ref, b_ref, m_ref, o_ref, p_ref):
    a = half_of(a_ref, core_ref[0])
    b = b_ref[...]
    s = s_ref[...].reshape(1024, 512)
    rate = 1.0 / (1.0 + m_ref[0:1, 0:1] * (1.0 / 8388608.0))
    for ref, out, base, k in ((q_ref, o_ref, a, 0), (r_ref, p_ref, b, 1)):
        combined = n_ref[k] + jnp.dot(joined(ref), s, preferred_element_type=f32)
        out[...] = ((1.0 + rate) * base.astype(f32) - (rate * (1.0 / 1024.0)) * combined).astype(bf16)


def join_body(core_ref, mine_ref, theirs_ref, o_ref, sems):
    def join(left_ref, right_ref):
        left = pltpu.make_async_copy(left_ref, o_ref.at[:, 0:512], sems.at[0])
        right = pltpu.make_async_copy(right_ref, o_ref.at[:, 512:1024], sems.at[1])
        left.start()
        right.start()
        left.wait()
        right.wait()

    @pl.when(core_ref[0] == 0)
    def _():
        join(mine_ref, theirs_ref)

    @pl.when(core_ref[0] == 1)
    def _():
        join(theirs_ref, mine_ref)


def shards(factors, owner, grads):
    core = lax.axis_index("core")
    cores = core[None].astype(jnp.int32)
    quarter = 2 * core + lax.axis_index("z") % 2
    rows = gradient_quarters(grads, quarter)
    plan, received = scatter_columns(factors[0], owner[0], quarter)
    tiles = shape((8, 512, 128))
    own, projected = with_panel(project_body, (shape((512, 1024)), tiles), plan, factors[0], *rows, *received)
    projected = exchange(projected, GROUP)
    projected = exchange(call(spread_body, tiles, projected), GROUP)
    given = flip(call(give_body, tiles, cores, own, projected, scalars=1), "core")
    kept = call(keep_body, tiles, cores, own, projected, given, scalars=1)
    other_own = flip(lax.dynamic_slice_in_dim(own, (1 - core) * 512, 512, 1), "core")
    piece = call(total_body, shape((512, 128)), exchange(kept, CHIP))
    swap = []
    for x in range(4):
        for yh in range(2):
            for yl in range(2):
                for z in range(4):
                    g, c = x * 2 + yh, yl * 4 + z
                    swap.append((g * 8 + c, c * 8 + g))
    piece = lax.ppermute(piece, GROUP_CHIP, swap)
    precond = copies_to(piece, GROUP)
    other = flip(precond, "core")
    products = call(outer_body, shape((8, 144, 512)), cores, precond, other, own, other_own, scalars=1)
    near = call(near_body, shape((2, 512, 512), f32), cores, precond, other, own, other_own, scalars=1)
    products = exchange(products, CHIP)
    later, squares = call(suffix_body, (shape((8, 128, 512)), shape((8, 128), f32)), products)
    later = exchange(later, CHIP)
    half = shape((512, 512))
    mine, theirs = call(
        update_body, (half, half), cores, precond, other, later, near, own, other_own, squares, scalars=1
    )
    theirs = flip(theirs, "core")
    return pl.pallas_call(
        join_body,
        out_shape=shape((512, 1024)),
        in_specs=[pl.BlockSpec(memory_space=pltpu.SMEM)] + [pl.BlockSpec(memory_space=pltpu.VMEM)] * 2,
        out_specs=pl.BlockSpec(memory_space=pl.ANY),
        scratch_shapes=[pltpu.SemaphoreType.DMA((2,))],
        compiler_params=params,
    )(cores, mine, theirs)


def solution(mesh):
    split = Mesh(mesh.devices.reshape(4, 2, 2, 4, 2), GROUP + MEMBER)
    in_specs = (P(GROUP, MEMBER, None), P(), P(None, GROUP))
    out_specs = P(MEMBER, GROUP)
    return jax.shard_map(shards, mesh=split, in_specs=in_specs, out_specs=out_specs, check_vma=False)
```

```python
import jax
import jax.numpy as jnp
from jax import lax
from jax.experimental import pallas as pl
from jax.experimental.pallas import tpu as pltpu
from jax.sharding import Mesh
from jax.sharding import PartitionSpec as P

GROUP = ("x", "yh")
CHIP = ("yl", "z")
MEMBER = ("yl", "z", "core")
GROUP_CHIP = GROUP + CHIP
bf16 = jnp.bfloat16
f32 = jnp.float32
params = pltpu.CompilerParams(vmem_limit_bytes=48 * 1024 * 1024)


def call(body, out, *args, scalars=0, scratch=()):
    vmem = pl.BlockSpec(memory_space=pltpu.VMEM)
    smem = pl.BlockSpec(memory_space=pltpu.SMEM)
    specs = [smem] * scalars + [vmem] * (len(args) - scalars)
    return pl.pallas_call(
        body,
        out_shape=out,
        in_specs=specs,
        out_specs=jax.tree.map(lambda _: vmem, out),
        scratch_shapes=scratch,
        compiler_params=params,
    )(*args)


def shape(dims, dtype=bf16):
    return jax.ShapeDtypeStruct(dims, dtype)


def contract(left, right, a, b):
    return lax.dot_general(left, right, (((a,), (b,)), ((), ())), preferred_element_type=f32)


def joined(ref):
    return jnp.concatenate([ref[b] for b in range(8)], axis=1)


def shift_x(value, step):
    return lax.ppermute(value, "x", [(i, (i + step) % 4) for i in range(4)])


def flip(value, axis):
    return lax.ppermute(value, axis, [(0, 1), (1, 0)])


def copies_to(value, axes):
    return lax.all_to_all(jnp.broadcast_to(value, (8, *value.shape)), axes, 0, 0, tiled=True)


def exchange(tiles, axes):
    return lax.all_to_all(tiles, axes, 0, 0, tiled=True)


def copy_blocks(panel_ref, sems, *pairs):
    copies = []
    for column, out_ref in pairs:
        start = pl.multiple_of(column * 1024, 1024)
        for top in range(0, out_ref.shape[0], 128):
            source = panel_ref.at[pl.ds(top, 128), pl.ds(start, 1024)]
            copies.append(pltpu.make_async_copy(source, out_ref.at[pl.ds(top, 128)], sems.at[len(copies)]))
    for copy in copies:
        copy.start()
    for copy in copies:
        copy.wait()


FAR, DOWN, RIGHT, LEFT, HERE, QUARTER = 2, 3, 4, 5, 6, 7


def cross_body(plan_ref, panel_ref, right_ref, left_ref, cross_ref, sems):
    @pl.when(plan_ref[0] == 0)
    def _():
        copy_blocks(panel_ref, sems, (plan_ref[DOWN], cross_ref))

    @pl.when(plan_ref[0] == 1)
    def _():
        cross_ref[...] = right_ref[...]

    @pl.when(plan_ref[0] > 1)
    def _():
        cross_ref[...] = left_ref[...]


def far_body(plan_ref, panel_ref, across_ref, upper_ref, lower_ref, far_ref, sems):
    @pl.when(plan_ref[1] == 0)
    def _():
        copy_blocks(panel_ref, sems, (plan_ref[FAR], far_ref))
        upper_ref[...] = far_ref[:256]
        lower_ref[...] = far_ref[256:]

    @pl.when(plan_ref[1] == 1)
    def _():
        upper_ref[...] = across_ref[:256]
        lower_ref[...] = across_ref[256:]


def third_body(plan_ref, panel_ref, right_ref, left_ref, to_right_ref, to_left_ref, sems):
    @pl.when(plan_ref[0] == 0)
    def _():
        copy_blocks(panel_ref, sems, (plan_ref[RIGHT], to_right_ref), (plan_ref[LEFT], to_left_ref))

    @pl.when(plan_ref[0] > 0)
    def _():
        to_right_ref[...] = right_ref[...]
        to_left_ref[...] = left_ref[...]


def with_panel(body, out, plan, panel, *received, scratch=()):
    vmem = pl.BlockSpec(memory_space=pltpu.VMEM)
    return pl.pallas_call(
        body,
        out_shape=out,
        in_specs=[pl.BlockSpec(memory_space=pltpu.SMEM), pl.BlockSpec(memory_space=pl.ANY)] + [vmem] * len(received),
        out_specs=jax.tree.map(lambda _: vmem, out),
        scratch_shapes=(*scratch, pltpu.SemaphoreType.DMA((8,))),
        compiler_params=params,
    )(plan, panel, *received)


def scatter_columns(panel, owner, quarter):
    rx = (lax.axis_index("x") - owner // 2) % 4
    ry = (lax.axis_index("yh") - owner % 2) % 2

    def column(i, j):
        return ((owner // 2 + i) % 4) * 2 + (owner % 2 + j) % 2

    def block(i, j):
        return lax.dynamic_slice_in_dim(panel, column(i, j) * 1024, 1024, 1)

    places = [column(2, 0), column(0, 1), column(1, 0), column(3, 0), column(0, 0)]
    plan = jnp.stack([rx, ry, *places, quarter]).astype(jnp.int32)
    full, half = shape((512, 1024)), shape((256, 1024))
    to_right = shift_x(block(1, 1), 1)
    to_left = shift_x(block(3, 1), 3)
    across = flip(block(2, 1), "yh")
    lower_right = shift_x(block(1, 0)[256:], 1)
    lower_left = shift_x(block(3, 0)[256:], 3)
    crossing = flip(with_panel(cross_body, full, plan, panel, to_right, to_left), "yh")
    upper, lower = with_panel(
        far_body, (half, half), plan, panel, across, scratch=(pltpu.VMEM((512, 1024), bf16),)
    )
    far_right = shift_x(upper, 1)
    far_left = shift_x(lower, 3)
    upper_right, upper_left = with_panel(third_body, (half, half), plan, panel, far_right, far_left)
    return plan, (shift_x(upper_right, 1), lower_right, shift_x(upper_left, 3), lower_left, crossing)


def quarter_body(plan_ref, g_ref, o_ref):
    pltpu.sync_copy(g_ref.at[:, plan_ref[0]], o_ref)


def gradient_quarters(grads, quarter):
    piece = pl.pallas_call(
        quarter_body,
        out_shape=shape((8, 256, 128)),
        in_specs=[pl.BlockSpec(memory_space=pltpu.SMEM), pl.BlockSpec(memory_space=pl.ANY)],
        out_specs=pl.BlockSpec(memory_space=pltpu.VMEM),
    )(quarter[None].astype(jnp.int32), grads.reshape(8, 4, 256, 128))
    mine = exchange(piece, GROUP)
    near = lax.ppermute(mine, "z", [(0, 1), (1, 0), (2, 3), (3, 2)])
    return mine, near, flip(mine, "core"), flip(near, "core")


def project_body(plan_ref, panel_ref, g0_ref, g1_ref, g2_ref, g3_ref, *refs):
    upper_right, lower_right, upper_left, lower_left, across_ref, a_ref, o_ref, sems = refs
    column, row = plan_ref[0], plan_ref[1]
    straight = row == 0

    @pl.when((column == 0) & straight)
    def _():
        copy_blocks(panel_ref, sems, (plan_ref[HERE], a_ref))

    @pl.when((column == 1) & straight)
    def _():
        a_ref[:256] = upper_right[...]
        a_ref[256:] = lower_right[...]

    @pl.when((column == 3) & straight)
    def _():
        a_ref[:256] = upper_left[...]
        a_ref[256:] = lower_left[...]

    @pl.when(column == 2)
    def _():
        a_ref[:256] = upper_right[...]
        a_ref[256:] = upper_left[...]

    @pl.when((column != 2) & (row == 1))
    def _():
        a_ref[...] = across_ref[...]

    quarter = plan_ref[QUARTER]
    half = 2 * (quarter // 2)
    place = quarter - half
    columns = (quarter, half + 1 - place, 2 - half + place, 2 - half + 1 - place)
    parts = [a_ref[:, pl.ds(pl.multiple_of(k * 256, 256), 256)] for k in columns]
    for j in range(4):
        value = jnp.zeros((512, 256), f32)
        for part, ref in zip(parts, (g0_ref, g1_ref, g2_ref, g3_ref)):
            rows = jnp.concatenate([ref[2 * j], ref[2 * j + 1]], axis=1)
            value = value + jnp.dot(part, rows, preferred_element_type=f32)
        o_ref[2 * j] = value[:, :128].astype(bf16)
        o_ref[2 * j + 1] = value[:, 128:].astype(bf16)


def spread_body(t_ref, o_ref):
    total = t_ref[0].astype(f32)
    for k in range(1, 8):
        total = total + t_ref[k].astype(f32)
    total = total.astype(bf16)
    for k in range(8):
        o_ref[k] = total


def total_body(t_ref, o_ref):
    total = t_ref[0].astype(f32)
    for k in range(1, 8):
        total = total + t_ref[k].astype(f32)
    o_ref[...] = total.astype(bf16)


def half_of(a_ref, half):
    return a_ref[:, pl.ds(pl.multiple_of(half * 512, 512), 512)]


def give_body(core_ref, a_ref, p_ref, o_ref):
    a = half_of(a_ref, 1 - core_ref[0])
    for j in range(4):
        p = jnp.concatenate([p_ref[2 * j], p_ref[2 * j + 1]], axis=1)
        value = contract(a, p, 0, 0)
        o_ref[2 * j] = value[:, :128].astype(bf16)
        o_ref[2 * j + 1] = value[:, 128:].astype(bf16)


def keep_body(core_ref, a_ref, p_ref, r_ref, o_ref):
    a = half_of(a_ref, core_ref[0])
    for j in range(4):
        p = jnp.concatenate([p_ref[2 * j], p_ref[2 * j + 1]], axis=1)
        value = contract(a, p, 0, 0)
        o_ref[2 * j] = (value[:, :128] + r_ref[2 * j].astype(f32)).astype(bf16)
        o_ref[2 * j + 1] = (value[:, 128:] + r_ref[2 * j + 1].astype(f32)).astype(bf16)


def squares_of(value):
    wide = value.astype(f32)
    return jnp.sum((wide * wide).reshape(64, 8, 2, 128), axis=(0, 2))


def outer_own_body(core_ref, q_ref, a_ref, o_ref, s_ref):
    a = half_of(a_ref, core_ref[0])
    squares = jnp.zeros((8, 128), f32)
    for j in range(4):
        q = jnp.concatenate([q_ref[2 * j], q_ref[2 * j + 1]], axis=1)
        o_ref[256 * j : 256 * j + 256] = contract(q, a, 0, 0)
        squares = squares + squares_of(q)
    s_ref[...] = squares


def outer_body(p_ref, s_ref, r_ref, b_ref, o_ref):
    b = b_ref[...]
    squares = s_ref[...]
    for j in range(4):
        r = jnp.concatenate([r_ref[2 * j], r_ref[2 * j + 1]], axis=1)
        value = (p_ref[256 * j : 256 * j + 256] + contract(r, b, 0, 0)).astype(bf16)
        o_ref[2 * j, :128] = value[:128]
        o_ref[2 * j + 1, :128] = value[128:]
        squares = squares + squares_of(r)
    total = jnp.broadcast_to(jnp.sum(squares, axis=(0, 1), keepdims=True), (16, 512))
    top = total.astype(bf16)
    rest = total - top.astype(f32)
    middle = rest.astype(bf16)
    bottom = (rest - middle.astype(f32)).astype(bf16)
    row = lax.broadcasted_iota(jnp.int32, (16, 512), 0)
    tail = jnp.where(row == 0, top.astype(f32), jnp.where(row == 1, middle.astype(f32), bottom.astype(f32)))
    for j in range(8):
        o_ref[j, 128:] = tail.astype(bf16)


def suffix_body(t_ref, o_ref, s_ref):
    total = jnp.zeros((128, 512), f32)
    squares = jnp.zeros((1, 128), f32)
    for k in reversed(range(8)):
        o_ref[k] = total.astype(bf16)
        total = total + t_ref[k, :128].astype(f32)
        tail = t_ref[k, 128:, :128].astype(f32)
        squares = squares + (tail[0:1] + tail[1:2] + tail[2:3])
    s_ref[...] = jnp.broadcast_to(squares, (8, 128))


def near_body(core_ref, q_ref, r_ref, a_ref, b_ref, o_ref):
    core = core_ref[0]
    q = joined(q_ref)
    r = joined(r_ref)
    a = half_of(a_ref, core)
    b = b_ref[...]

    def times(gram, rows):
        top = gram.astype(bf16)
        rest = (gram - top.astype(f32)).astype(bf16)
        return jnp.dot(top, rows, preferred_element_type=f32) + jnp.dot(rest, rows, preferred_element_type=f32)

    upper = lax.broadcasted_iota(jnp.int32, (512, 512), 0) <= lax.broadcasted_iota(jnp.int32, (512, 512), 1)
    o_ref[0] = times(jnp.where(upper, contract(q, q, 1, 1), 0.0), a)
    o_ref[1] = times(jnp.where(upper, contract(r, r, 1, 1), 0.0), b)

    @pl.when(core == 0)
    def _():
        o_ref[0] += times(contract(q, r, 1, 1), b)

    @pl.when(core == 1)
    def _():
        o_ref[1] += times(contract(r, q, 1, 1), a)


def update_body(core_ref, q_ref, r_ref, s_ref, n_ref, a_ref, b_ref, m_ref, o_ref, p_ref):
    a = half_of(a_ref, core_ref[0])
    b = b_ref[...]
    s = s_ref[...].reshape(1024, 512)
    rate = 1.0 / (1.0 + m_ref[0:1, 0:1] * (1.0 / 8388608.0))
    for ref, out, base, k in ((q_ref, o_ref, a, 0), (r_ref, p_ref, b, 1)):
        combined = n_ref[k] + jnp.dot(joined(ref), s, preferred_element_type=f32)
        out[...] = ((1.0 + rate) * base.astype(f32) - (rate * (1.0 / 1024.0)) * combined).astype(bf16)


def join_body(core_ref, mine_ref, theirs_ref, o_ref, sems):
    def join(left_ref, right_ref):
        left = pltpu.make_async_copy(left_ref, o_ref.at[:, 0:512], sems.at[0])
        right = pltpu.make_async_copy(right_ref, o_ref.at[:, 512:1024], sems.at[1])
        left.start()
        right.start()
        left.wait()
        right.wait()

    @pl.when(core_ref[0] == 0)
    def _():
        join(mine_ref, theirs_ref)

    @pl.when(core_ref[0] == 1)
    def _():
        join(theirs_ref, mine_ref)


def shards(factors, owner, grads):
    core = lax.axis_index("core")
    cores = core[None].astype(jnp.int32)
    quarter = 2 * core + lax.axis_index("z") % 2
    rows = gradient_quarters(grads, quarter)
    plan, received = scatter_columns(factors[0], owner[0], quarter)
    tiles = shape((8, 512, 128))
    own, projected = with_panel(project_body, (shape((512, 1024)), tiles), plan, factors[0], *rows, *received)
    projected = exchange(projected, GROUP)
    projected = exchange(call(spread_body, tiles, projected), GROUP)
    given = flip(call(give_body, tiles, cores, own, projected, scalars=1), "core")
    kept = call(keep_body, tiles, cores, own, projected, given, scalars=1)
    other_own = flip(lax.dynamic_slice_in_dim(own, (1 - core) * 512, 512, 1), "core")
    piece = call(total_body, shape((512, 128)), exchange(kept, CHIP))
    swap = []
    for x in range(4):
        for yh in range(2):
            for yl in range(2):
                for z in range(4):
                    g, c = x * 2 + yh, yl * 4 + z
                    swap.append((g * 8 + c, c * 8 + g))
    piece = lax.ppermute(piece, GROUP_CHIP, swap)
    precond = copies_to(piece, GROUP)
    other = flip(precond, "core")
    partial = call(
        outer_own_body, (shape((1024, 512), f32), shape((8, 128), f32)), cores, precond, own, scalars=1
    )
    products = call(outer_body, shape((8, 144, 512)), *partial, other, other_own)
    near = call(near_body, shape((2, 512, 512), f32), cores, precond, other, own, other_own, scalars=1)
    products = exchange(products, CHIP)
    later, squares = call(suffix_body, (shape((8, 128, 512)), shape((8, 128), f32)), products)
    later = exchange(later, CHIP)
    half = shape((512, 512))
    mine, theirs = call(
        update_body, (half, half), cores, precond, other, later, near, own, other_own, squares, scalars=1
    )
    theirs = flip(theirs, "core")
    return pl.pallas_call(
        join_body,
        out_shape=shape((512, 1024)),
        in_specs=[pl.BlockSpec(memory_space=pltpu.SMEM)] + [pl.BlockSpec(memory_space=pltpu.VMEM)] * 2,
        out_specs=pl.BlockSpec(memory_space=pl.ANY),
        scratch_shapes=[pltpu.SemaphoreType.DMA((2,))],
        compiler_params=params,
    )(cores, mine, theirs)


def solution(mesh):
    split = Mesh(mesh.devices.reshape(4, 2, 2, 4, 2), GROUP + MEMBER)
    in_specs = (P(GROUP, MEMBER, None), P(), P(None, GROUP))
    out_specs = P(MEMBER, GROUP)
    return jax.shard_map(shards, mesh=split, in_specs=in_specs, out_specs=out_specs, check_vma=False)
```
